256 devices in a mesh: tm: 32 (over x, y, core), ens: 8 (over z).
Axes of the slice: x: 4, y: 4, z: 8, core: 2. Of those that a mesh axis runs over, the one named last changes fastest.
Arguments:
- propagators: float32 [8, 32, 512, 512], P('ens', 'tm'), may hold values from -1 to 1, as said below
- weights: float32 [8], P('ens'), may hold values from 2 to 8
- target: float32 [512, 512], replicated, may hold values from -1 to 1, as said below
Outputs:
- gradient: float32 [512, 32, 512], P('ens', 'tm')
The draws below stay inside these ranges and needn't reach their ends.
Inputs may be any that keep to these rules, and one draw needn't show every extreme that they name: Every propagators[m, t] is an orthogonal 512 x 512 matrix up to float32 rounding. target is an orthogonal 512 x 512 matrix up to float32 rounding.
All inputs are finite; a program needn't handle non-finite values.
Results may differ from the reference program's by a relative error of at most 0.0003.
Values sent between devices are 32-bit elements; how exact they have to be, the bound alone decides.
A program may use at most 128 MiB of HBM per device.

```python
import math
import jax
import jax.numpy as jnp
from jax import lax

R = 512
NT = 32
MEMBERS = 8


def cayley(seed_key, spread):
    gaussian = jax.random.normal(seed_key, (R, R), jnp.float32) * (spread / math.sqrt(2.0 * R))
    skew_part = gaussian - gaussian.T
    identity = jnp.eye(R, dtype=jnp.float32)
    return jnp.linalg.solve(identity - skew_part, identity + skew_part)


def draw_propagators(key, part):
    spread = 0.8
    how_many = MEMBERS * NT

    def single(slot_index):
        return cayley(jax.random.fold_in(key, slot_index), spread)
    matrices = lax.map(single, jnp.arange(how_many, dtype=jnp.int32))
    return matrices.reshape(MEMBERS, NT, R, R)


def draw_target(key, part):
    spread = 1.0
    return cayley(jax.random.fold_in(key, 7919), spread)


def level_of(key, dims, split, low, high):
    def one(axis_at, blocks):
        draws = jax.random.uniform(jax.random.fold_in(jax.random.fold_in(key, 6), axis_at), (blocks,), jnp.float32, low / len(split), high / len(split))
        return jnp.repeat(jnp.exp(draws), dims[axis_at] // blocks).reshape((-1,) + (1,) * (len(dims) - axis_at - 1))

    level = one(*split[0])
    for cut in split[1:]:
        level = level * one(*cut)
    return level


def setup_inputs(seed: int = 0) -> dict:
    splits = jax.random.split(jax.random.key(seed), 4)
    propagators = draw_propagators(jax.random.fold_in(splits[3], 71), 0)
    weights = jnp.clip(jnp.exp(math.log(8.0) - 1.3862944 * jax.random.uniform(splits[1], (MEMBERS,), jnp.float32) ** level_of(splits[1], (MEMBERS,), ((0, 8),), -0.2, 0.2)), 2.0, 8.0)
    target = draw_target(jax.random.fold_in(splits[3], 71), 0)
    return {"propagators": propagators, "weights": weights, "target": target}


highest = lax.Precision.HIGHEST

def reference(propagators, weights, target):
    identity = jnp.eye(R, dtype=jnp.float32)

    def member(running_sum, inputs):
        member_slices, weight = inputs

        def advance(running, factor):
            running = jnp.dot(factor.astype(jnp.float32), running.astype(jnp.float32), precision=highest, preferred_element_type=jnp.float32)
            return (running, running)
        final_product, stacked = lax.scan(advance, identity, member_slices)
        twisted = jnp.dot(target.T.astype(jnp.float32), final_product.astype(jnp.float32), precision=highest, preferred_element_type=jnp.float32)
        skew_part = weight * (twisted - twisted.T) * 0.5
        right_factor = jnp.einsum('ij,tkj->tik', skew_part, stacked, precision=highest)
        member_term = jnp.einsum('tik,tkj->itj', stacked, right_factor, precision=highest)
        return (running_sum + member_term, None)
    zeros_init = jnp.zeros((R, NT, R), jnp.float32)
    summed, _ = lax.scan(member, zeros_init, (propagators, weights))
    return summed
```

```python
import jax
import jax.numpy as jnp
from jax import lax
from jax.sharding import PartitionSpec as P

highest = lax.Precision.HIGHEST


def shards(propagators, weights, target):
    slot = lax.axis_index("tm")
    slices = lax.axis_size("tm")
    own = propagators[0, 0]
    first = jnp.dot(own, target.T, precision=highest)
    window = jnp.where(slot == 0, first, own)
    step = 1
    while step < slices:
        ring = [(i, (i + step) % slices) for i in range(slices)]
        earlier = lax.ppermute(window, "tm", ring)
        window = jnp.dot(window, earlier, precision=highest)
        step *= 2
    term = (0.5 * weights[0]) * (window - window.T)
    summed = lax.psum_scatter(term, "ens", scatter_dimension=0, tiled=True)
    return summed[:, None, :]


def solution(mesh):
    placed = (P("ens", "tm", None, None), P("ens"), P())
    return jax.shard_map(
        shards, mesh=mesh, in_specs=placed, out_specs=P("ens", "tm", None), check_vma=False
    )
```

```python
import functools

import jax
import jax.numpy as jnp
from jax import lax
from jax.experimental import pallas as pl
from jax.experimental.pallas import tpu as pltpu
from jax.sharding import PartitionSpec as P

MESH = pl.DeviceIdType.MESH
R = 512
HALF = R // 2
PIECE = 128
SMALL = 64
ROWS = 64
CHUNK = 16
COPIES = 96


def split(value):
    high = value.astype(jnp.bfloat16)
    low = (value - high.astype(jnp.float32)).astype(jnp.bfloat16)
    return high, low


def kernel(
    prop_ref, target_ref, weight_ref, out_ref,
    pair, target, chips, halves, rows, left, right, va, vb, mid, grad,
    long_in, short_in, bh, bl, send_sem, recv_sem, local_sem,
):
    slot = lax.axis_index("tm")
    z = lax.axis_index("ens")
    core = lax.rem(slot, 2)
    y = lax.rem(slot // 2, 4)
    x = slot // 8

    def at(x_, y_, core_):
        return ((x_ * 4 + y_) * 2 + core_, z)

    xp, xm, xo = lax.rem(x + 1, 4), lax.rem(x + 3, 4), lax.rem(x + 2, 4)
    yp, ym, yo = lax.rem(y + 1, 4), lax.rem(y + 3, 4), lax.rem(y + 2, 4)
    sibling = at(x, y, 1 - core)
    to_yp, to_ym = at(x, yp, core), at(x, ym, core)
    to_xp, to_xm = at(xp, y, core), at(xm, y, core)
    to_long = (slot, lax.rem(z + 1 + 6 * core, 8))
    to_short = (slot, lax.rem(z + 7 - 6 * core, 8))

    own_load = pltpu.make_async_copy(prop_ref, pair.at[core], local_sem.at[0])
    own_load.start()
    target_load = pltpu.make_async_copy(target_ref, target, local_sem.at[1])
    target_load.start()

    barrier = pltpu.get_barrier_semaphore()
    peers = (sibling, to_yp, to_ym, to_xp, to_xm, to_long, to_short)
    for peer in peers:
        pl.semaphore_signal(barrier, inc=1, device_id=peer, device_id_type=MESH)
    pl.semaphore_wait(barrier, len(peers))

    started = []

    def send(src, dst, device):
        n = len(started)
        copy = pltpu.make_async_remote_copy(
            src_ref=src, dst_ref=dst, send_sem=send_sem.at[n], recv_sem=recv_sem.at[n],
            device_id=device, device_id_type=MESH,
        )
        copy.start()
        started.append(copy)
        return copy

    def prepare(b):
        high, low = split(b[...])
        bh[...] = high
        bl[...] = low

    def product_rows(dst, a, start, count, nt=False):
        dims = (((1,), (1 if nt else 0,)), ((), ()))

        def dot(p, q):
            return lax.dot_general(p, q, dims, preferred_element_type=jnp.float32)

        block = pl.ds(start, count)
        high, low = split(a[block, :])
        dst[block, :] = dot(high, bh[...]) + (dot(high, bl[...]) + dot(low, bh[...]))

    def product(dst, a, b, nt=False):
        prepare(b)

        def one(i, _):
            product_rows(dst, a, pl.multiple_of(i * HALF, HALF), HALF, nt)
            return 0

        lax.fori_loop(0, 2, one, 0)

    swap = send(prop_ref, pair.at[core], sibling)
    own_load.wait()
    target_load.wait()
    swap.wait_recv()

    @pl.when(slot // 2 == 0)
    def _():
        product(pair.at[0], pair.at[0], target, nt=True)

    mine = pl.multiple_of(core * HALF, HALF)
    other = pl.multiple_of((1 - core) * HALF, HALF)
    first, second = pl.ds(mine, PIECE), pl.ds(mine + PIECE, PIECE)
    prepare(pair.at[0])
    own = chips.at[y]
    product_rows(own, pair.at[1], mine, PIECE)
    up0 = send(own.at[first], own.at[first], to_yp)
    product_rows(own, pair.at[1], pl.multiple_of(mine + PIECE, PIECE), PIECE)
    down0 = send(own.at[second], own.at[second], to_ym)
    up1 = send(own.at[second], own.at[second], to_yp)
    down1 = send(own.at[first], own.at[first], to_ym)
    product_rows(own, pair.at[1], other, HALF)

    def pass_on(ref, block):
        return send(ref.at[block], ref.at[block], sibling)

    up0.wait_recv()
    up2 = send(chips.at[ym].at[first], chips.at[ym].at[first], to_yp)
    near = [pass_on(chips.at[ym], first)]
    down0.wait_recv()
    down2 = send(chips.at[yp].at[second], chips.at[yp].at[second], to_ym)
    near.append(pass_on(chips.at[yp], second))
    up1.wait_recv()
    near.append(pass_on(chips.at[ym], second))
    down1.wait_recv()
    near.append(pass_on(chips.at[yp], first))
    for copy in near:
        copy.wait_recv()
    here = y // 2
    product(halves.at[here], chips.at[2 * here + 1], chips.at[2 * here])
    up2.wait_recv()
    far = [pass_on(chips.at[yo], first)]
    down2.wait_recv()
    far.append(pass_on(chips.at[yo], second))
    for copy in far:
        copy.wait_recv()
    product(halves.at[1 - here], chips.at[3 - 2 * here], chips.at[2 - 2 * here])

    half = lax.rem(y, 2)

    def piece(half_, number):
        return pl.ds(pl.multiple_of(half_ * HALF + number * SMALL, SMALL), SMALL)

    a_here, b_here = piece(half, core), piece(half, 2 + core)
    a_there, b_there = piece(1 - half, core), piece(1 - half, 2 + core)
    prepare(halves.at[0])
    row = rows.at[x]
    product_rows(row, halves.at[1], pl.multiple_of(half * HALF, HALF), HALF)
    xu_a = send(row.at[a_here], row.at[a_here], to_xp)
    xd_b = send(row.at[b_here], row.at[b_here], to_xm)
    xu_b = send(row.at[b_here], row.at[b_here], to_xp)
    xd_a = send(row.at[a_here], row.at[a_here], to_xm)
    product_rows(row, halves.at[1], pl.multiple_of((1 - half) * HALF, HALF), HALF)

    def take(copy, ref, block, onward):
        copy.wait_recv()
        return send(ref.at[block], ref.at[block], onward), pass_on(ref, block)

    xu_a.wait_recv()
    xu_r = send(rows.at[xm].at[a_here], rows.at[xm].at[a_here], to_xp)
    y1 = send(rows.at[xm].at[a_here], rows.at[xm].at[a_here], to_yp)
    by_sibling = [pass_on(rows.at[xm], a_here)]
    xd_b.wait_recv()
    xd_r = send(rows.at[xp].at[b_here], rows.at[xp].at[b_here], to_xm)
    y2 = send(rows.at[xp].at[b_here], rows.at[xp].at[b_here], to_ym)
    by_sibling.append(pass_on(rows.at[xp], b_here))
    y3, got = take(xu_b, rows.at[xm], b_here, to_ym)
    by_sibling.append(got)
    y4, got = take(xd_a, rows.at[xp], a_here, to_yp)
    by_sibling.append(got)

    left[...] = jnp.where(core == 0, pair[0], own[...])

    def extend(i, _):
        product(left, left, chips.at[y - 1 - i])
        return 0

    lax.fori_loop(0, y, extend, 0)
    product(right, row, left, nt=True)

    y5, got = take(xu_r, rows.at[xo], a_here, to_yp)
    last_sibling = [got]
    y6, got = take(xd_r, rows.at[xo], b_here, to_ym)
    last_sibling.append(got)
    for copy, at_row, block in (
        (y1, xm, a_there), (y2, xp, b_there), (y3, xm, b_there), (y4, xp, a_there),
    ):
        copy.wait_recv()
        by_sibling.append(pass_on(rows.at[at_row], block))
    for copy in by_sibling:
        copy.wait_recv()
    product(va, left, rows.at[xm])
    product(vb, rows.at[xp], right)
    for copy, block in ((y5, a_there), (y6, b_there)):
        copy.wait_recv()
        last_sibling.append(pass_on(rows.at[xo], block))
    for copy in last_sibling:
        copy.wait_recv()
    product(mid, rows.at[xo], vb)
    product(right, va, mid)
    scale = 0.5 * weight_ref[0]
    turned = right[...]
    grad[...] = scale * (turned - turned.T)

    chunks = ROWS // CHUNK

    def own_rows(owner, q):
        return pl.ds(pl.multiple_of(owner * ROWS + q * CHUNK, CHUNK), CHUNK)

    def owner_long(step):
        return lax.rem(z + (4 - step) + core * 2 * (4 + step), 8)

    def owner_short(step):
        return lax.rem(z + 5 + step + core * 2 * (3 - step), 8)

    long_copies, short_copies = [], []
    for step in range(4):
        for q in range(chunks):
            spot = pl.ds(q * CHUNK, CHUNK)
            block = own_rows(owner_long(step), q)
            if step == 0:
                src = grad.at[block]
            else:
                long_copies[(step - 1) * chunks + q].wait_recv()
                src = long_in.at[step - 1].at[spot]
                src[...] += grad[block, :]
            long_copies.append(send(src, long_in.at[step].at[spot], to_long))
            if step == 3:
                continue
            block = own_rows(owner_short(step), q)
            if step == 0:
                src = grad.at[block]
            else:
                short_copies[(step - 1) * chunks + q].wait_recv()
                src = short_in.at[step - 1].at[spot]
                src[...] += grad[block, :]
            short_copies.append(send(src, short_in.at[step].at[spot], to_short))
    for q in range(chunks):
        spot = pl.ds(q * CHUNK, CHUNK)
        short_copies[2 * chunks + q].wait_recv()
        long_copies[3 * chunks + q].wait_recv()
        out_ref[spot, :] = (
            grad[own_rows(z, q), :] + long_in[3, spot, :] + short_in[2, spot, :]
        )
    for copy in started:
        copy.wait_send()
    assert len(started) <= COPIES


def shards(propagators, weights, target):
    full = pltpu.VMEM((R, R), jnp.float32)
    summed = pl.pallas_call(
        kernel,
        out_shape=jax.ShapeDtypeStruct((ROWS, R), jnp.float32),
        in_specs=[
            pl.BlockSpec(memory_space=pl.ANY),
            pl.BlockSpec(memory_space=pl.ANY),
            pl.BlockSpec(memory_space=pltpu.SMEM),
        ],
        out_specs=pl.BlockSpec(memory_space=pltpu.VMEM),
        scratch_shapes=[
            pltpu.VMEM((2, R, R), jnp.float32),
            full,
            pltpu.VMEM((4, R, R), jnp.float32),
            pltpu.VMEM((2, R, R), jnp.float32),
            pltpu.VMEM((4, R, R), jnp.float32),
            full, full, full, full, full, full,
            pltpu.VMEM((4, ROWS, R), jnp.float32),
            pltpu.VMEM((3, ROWS, R), jnp.float32),
            pltpu.VMEM((R, R), jnp.bfloat16),
            pltpu.VMEM((R, R), jnp.bfloat16),
            pltpu.SemaphoreType.DMA((COPIES,)),
            pltpu.SemaphoreType.DMA((COPIES,)),
            pltpu.SemaphoreType.DMA((2,)),
        ],
        compiler_params=pltpu.CompilerParams(
            collective_id=0, has_side_effects=True, vmem_limit_bytes=56 * 1024 * 1024
        ),
        name="grape",
    )(propagators[0, 0], target, weights)
    return summed[:, None, :]


def solution(mesh):
    placed = (P("ens", "tm", None, None), P("ens"), P())
    return jax.shard_map(
        shards, mesh=mesh, in_specs=placed, out_specs=P("ens", "tm", None), check_vma=False
    )
```

```python
import functools

import jax
import jax.numpy as jnp
from jax import lax
from jax.experimental import pallas as pl
from jax.experimental.pallas import tpu as pltpu
from jax.sharding import PartitionSpec as P

MESH = pl.DeviceIdType.MESH
R = 512
HALF = R // 2
PIECE = 128
SMALL = 64
SUB = 32
ROWS = 64
CHUNK = 16
COPIES = 160


def split(value):
    high = value.astype(jnp.bfloat16)
    low = (value - high.astype(jnp.float32)).astype(jnp.bfloat16)
    return high, low


def kernel(
    prop_ref, target_ref, weight_ref, out_ref,
    ends, target, mats, rows, strip, va, vb, mid, full, grad,
    long_in, short_in, bh, bl, send_sem, recv_sem, local_sem,
):
    slot = lax.axis_index("tm")
    z = lax.axis_index("ens")
    core = lax.rem(slot, 2)
    y = lax.rem(slot // 2, 4)
    x = slot // 8

    def at(x_, y_, core_):
        return ((x_ * 4 + y_) * 2 + core_, z)

    xp, xm, xo = lax.rem(x + 1, 4), lax.rem(x + 3, 4), lax.rem(x + 2, 4)
    yp, ym, yo = lax.rem(y + 1, 4), lax.rem(y + 3, 4), lax.rem(y + 2, 4)
    sibling = at(x, y, 1 - core)
    to_yp, to_ym = at(x, yp, core), at(x, ym, core)
    to_xp, to_xm = at(xp, y, core), at(xm, y, core)
    to_long = (slot, lax.rem(z + 1 + 6 * core, 8))
    to_short = (slot, lax.rem(z + 7 - 6 * core, 8))

    own_load = pltpu.make_async_copy(prop_ref, ends.at[core], local_sem.at[0])
    own_load.start()
    target_load = pltpu.make_async_copy(target_ref, target, local_sem.at[1])
    target_load.start()

    barrier = pltpu.get_barrier_semaphore()
    peers = (sibling, to_yp, to_ym, to_xp, to_xm, to_long, to_short)
    for peer in peers:
        pl.semaphore_signal(barrier, inc=1, device_id=peer, device_id_type=MESH)
    pl.semaphore_wait(barrier, len(peers))

    started = []

    def send(src, dst, device):
        n = len(started)
        copy = pltpu.make_async_remote_copy(
            src_ref=src, dst_ref=dst, send_sem=send_sem.at[n], recv_sem=recv_sem.at[n],
            device_id=device, device_id_type=MESH,
        )
        copy.start()
        started.append(copy)
        return copy

    def prepare(b):
        high, low = split(b[...])
        bh[...] = high
        bl[...] = low

    def product_rows(dst, a, start, count, nt=False):
        dims = (((1,), (1 if nt else 0,)), ((), ()))

        def dot(p, q):
            return lax.dot_general(p, q, dims, preferred_element_type=jnp.float32)

        block = pl.ds(start, count)
        high, low = split(a[block, :])
        dst[block, :] = dot(high, bh[...]) + (dot(high, bl[...]) + dot(low, bh[...]))

    def product(dst, a, b, nt=False):
        prepare(b)

        def one(i, _):
            product_rows(dst, a, pl.multiple_of(i * HALF, HALF), HALF, nt)
            return 0

        lax.fori_loop(0, 2, one, 0)

    swap = send(prop_ref, ends.at[core], sibling)
    own_load.wait()
    swap.wait_recv()
    mine = pl.multiple_of(core * HALF, HALF)
    other = pl.multiple_of((1 - core) * HALF, HALF)
    first, second = pl.ds(mine, PIECE), pl.ds(mine + PIECE, PIECE)
    prepare(ends.at[0])
    own = mats.at[y]
    product_rows(own, ends.at[1], mine, PIECE)
    up0 = send(own.at[first], own.at[first], to_yp)
    product_rows(own, ends.at[1], pl.multiple_of(mine + PIECE, PIECE), PIECE)
    down0 = send(own.at[second], own.at[second], to_ym)
    up1 = send(own.at[second], own.at[second], to_yp)
    down1 = send(own.at[first], own.at[first], to_ym)
    product_rows(own, ends.at[1], other, HALF)

    @pl.when(core == 1)
    def _():
        ends[0] = own[...]
        down = lax.broadcasted_iota(jnp.int32, (R, R), 0)
        across = lax.broadcasted_iota(jnp.int32, (R, R), 1)
        ends[1] = jnp.where(down == across, 1.0, 0.0).astype(jnp.float32)

    def pass_on(ref, block):
        return send(ref.at[block], ref.at[block], sibling)

    up0.wait_recv()
    up2 = send(mats.at[ym].at[first], mats.at[ym].at[first], to_yp)
    near = [pass_on(mats.at[ym], first)]
    down0.wait_recv()
    down2 = send(mats.at[yp].at[second], mats.at[yp].at[second], to_ym)
    near.append(pass_on(mats.at[yp], second))
    up1.wait_recv()
    near.append(pass_on(mats.at[ym], second))
    down1.wait_recv()
    near.append(pass_on(mats.at[yp], first))
    for copy in near:
        copy.wait_recv()
    late, odd = y // 2, lax.rem(y, 2)
    product(mats.at[4 + late], mats.at[2 * late + 1], mats.at[2 * late])

    @pl.when(odd == 0)
    def _():
        product(ends.at[2], mats.at[2 * late + 1], ends.at[1])

    @pl.when(odd == 1)
    def _():
        product(ends.at[2], ends.at[0], mats.at[2 * late])

    up2.wait_recv()
    far = [pass_on(mats.at[yo], first)]
    down2.wait_recv()
    far.append(pass_on(mats.at[yo], second))
    for copy in far:
        copy.wait_recv()

    subs = SMALL // SUB

    def pieces(half, number):
        start = half * HALF + number * SMALL
        return [pl.ds(pl.multiple_of(start + n * SUB, SUB), SUB) for n in range(subs)]

    a_here, b_here = pieces(odd, core), pieces(odd, 2 + core)
    a_there, b_there = pieces(1 - odd, core), pieces(1 - odd, 2 + core)
    begin = mats.at[3 + 2 * late]
    for n in range(subs):
        strip[n * SUB:(n + 1) * SUB, :] = begin[a_here[n], :]
        strip[SMALL + n * SUB:SMALL + (n + 1) * SUB, :] = begin[b_here[n], :]
    prepare(mats.at[2 - late])
    product_rows(strip, strip, 0, 2 * SMALL)
    prepare(mats.at[4 - 4 * late])
    product_rows(strip, strip, 0, 2 * SMALL)
    target_load.wait()

    @pl.when(x == 0)
    def _():
        prepare(target)
        product_rows(strip, strip, 0, 2 * SMALL, nt=True)

    strip_a = [strip.at[pl.ds(n * SUB, SUB)] for n in range(subs)]
    strip_b = [strip.at[pl.ds(SMALL + n * SUB, SUB)] for n in range(subs)]
    own_row = rows.at[x]
    xu_a, xd_b, xu_b, xd_a = [], [], [], []
    for n in range(subs):
        xu_a.append(send(strip_a[n], own_row.at[a_here[n]], to_xp))
        xd_b.append(send(strip_b[n], own_row.at[b_here[n]], to_xm))
    for n in range(subs):
        xu_b.append(send(strip_b[n], own_row.at[b_here[n]], to_xp))
        xd_a.append(send(strip_a[n], own_row.at[a_here[n]], to_xm))

    product(mats.at[5 - late], mats.at[3 - 2 * late], mats.at[2 - 2 * late])

    @pl.when(late == 0)
    def _():
        product(ends.at[3], mats.at[5], ends.at[2 - odd])

    @pl.when(late == 1)
    def _():
        product(ends.at[3], ends.at[2 * odd], mats.at[4])

    left = ends.at[(1 - late) * 2 * odd + late * 3]
    right = ends.at[(1 - late) * 3 + late * (2 - odd)]

    close_x, close_y, far_x, far_y = [], [], [], []
    onward, relays_u, relays_d = [], [], []

    def forward(copy, at_row, block, to_y, relay=None):
        copy.wait_recv()
        part = rows.at[at_row].at[block]
        relayed = None if relay is None else send(part, part, relay)
        return relayed, send(part, part, to_y), send(part, part, sibling)

    for n in range(subs):
        relayed, up, got = forward(xu_a[n], xm, a_here[n], to_yp, to_xp)
        relays_u.append(relayed)
        onward.append((up, xm, a_there[n]))
        close_x.append(got)
        relayed, up, got = forward(xd_b[n], xp, b_here[n], to_ym, to_xm)
        relays_d.append(relayed)
        onward.append((up, xp, b_there[n]))
        close_x.append(got)
    for n in range(subs):
        _, up, got = forward(xu_b[n], xm, b_here[n], to_ym)
        onward.append((up, xm, b_there[n]))
        close_x.append(got)
        _, up, got = forward(xd_a[n], xp, a_here[n], to_yp)
        onward.append((up, xp, a_there[n]))
        close_x.append(got)
    onward_far = []
    for n in range(subs):
        _, up, got = forward(relays_u[n], xo, a_here[n], to_yp)
        onward_far.append((up, a_there[n]))
        far_x.append(got)
        _, up, got = forward(relays_d[n], xo, b_here[n], to_ym)
        onward_far.append((up, b_there[n]))
        far_x.append(got)

    @pl.when(x == 0)
    def _():
        product(left, left, target, nt=True)

    def pass_some(some):
        for copy, at_row, block in some:
            copy.wait_recv()
            close_y.append(pass_on(rows.at[at_row], block))

    near_half = pl.multiple_of(odd * HALF, HALF)
    far_half = pl.multiple_of((1 - odd) * HALF, HALF)

    def add_half(dst, a, b, start, first):
        block = pl.ds(start, HALF)
        b_high, b_low = split(b[block, :])
        high, low = split(a[:, block])

        def dot(p, q):
            return jnp.dot(p, q, preferred_element_type=jnp.float32)

        value = dot(high, b_high) + (dot(high, b_low) + dot(low, b_high))
        dst[...] = value if first else dst[...] + value

    pass_some(onward[:2 * subs])
    for copy in close_x:
        copy.wait_recv()
    add_half(va, left, rows.at[xm], near_half, True)
    prepare(right)
    product_rows(vb, rows.at[xp], near_half, HALF)
    pass_some(onward[2 * subs:])
    for copy in close_y:
        copy.wait_recv()
    add_half(va, left, rows.at[xm], far_half, False)
    product_rows(vb, rows.at[xp], far_half, HALF)
    for copy, block in onward_far:
        copy.wait_recv()
        far_y.append(pass_on(rows.at[xo], block))
    for copy in far_x:
        copy.wait_recv()
    prepare(vb)
    product_rows(mid, rows.at[xo], near_half, HALF)
    add_half(full, va, mid, near_half, True)
    for copy in far_y:
        copy.wait_recv()
    product_rows(mid, rows.at[xo], far_half, HALF)
    add_half(full, va, mid, far_half, False)
    scale = 0.5 * weight_ref[0]
    turned = full[...]
    grad[...] = scale * (turned - turned.T)

    chunks = ROWS // CHUNK

    def own_rows(owner, q):
        return pl.ds(pl.multiple_of(owner * ROWS + q * CHUNK, CHUNK), CHUNK)

    def owner_long(step):
        return lax.rem(z + (4 - step) + core * 2 * (4 + step), 8)

    def owner_short(step):
        return lax.rem(z + 5 + step + core * 2 * (3 - step), 8)

    long_copies, short_copies = [], []
    for step in range(4):
        for q in range(chunks):
            spot = pl.ds(q * CHUNK, CHUNK)
            block = own_rows(owner_long(step), q)
            if step == 0:
                src = grad.at[block]
            else:
                long_copies[(step - 1) * chunks + q].wait_recv()
                src = long_in.at[step - 1].at[spot]
                src[...] += grad[block, :]
            long_copies.append(send(src, long_in.at[step].at[spot], to_long))
            if step == 3:
                continue
            block = own_rows(owner_short(step), q)
            if step == 0:
                src = grad.at[block]
            else:
                short_copies[(step - 1) * chunks + q].wait_recv()
                src = short_in.at[step - 1].at[spot]
                src[...] += grad[block, :]
            short_copies.append(send(src, short_in.at[step].at[spot], to_short))
    for q in range(chunks):
        spot = pl.ds(q * CHUNK, CHUNK)
        short_copies[2 * chunks + q].wait_recv()
        long_copies[3 * chunks + q].wait_recv()
        out_ref[spot, :] = (
            grad[own_rows(z, q), :] + long_in[3, spot, :] + short_in[2, spot, :]
        )
    for copy in started:
        copy.wait_send()
    assert len(started) <= COPIES


def shards(propagators, weights, target):
    full = pltpu.VMEM((R, R), jnp.float32)
    summed = pl.pallas_call(
        kernel,
        out_shape=jax.ShapeDtypeStruct((ROWS, R), jnp.float32),
        in_specs=[
            pl.BlockSpec(memory_space=pl.ANY),
            pl.BlockSpec(memory_space=pl.ANY),
            pl.BlockSpec(memory_space=pltpu.SMEM),
        ],
        out_specs=pl.BlockSpec(memory_space=pltpu.VMEM),
        scratch_shapes=[
            pltpu.VMEM((4, R, R), jnp.float32),
            full,
            pltpu.VMEM((6, R, R), jnp.float32),
            pltpu.VMEM((4, R, R), jnp.float32),
            pltpu.VMEM((2 * SMALL, R), jnp.float32),
            full, full, full, full, full,
            pltpu.VMEM((4, ROWS, R), jnp.float32),
            pltpu.VMEM((3, ROWS, R), jnp.float32),
            pltpu.VMEM((R, R), jnp.bfloat16),
            pltpu.VMEM((R, R), jnp.bfloat16),
            pltpu.SemaphoreType.DMA((COPIES,)),
            pltpu.SemaphoreType.DMA((COPIES,)),
            pltpu.SemaphoreType.DMA((2,)),
        ],
        compiler_params=pltpu.CompilerParams(
            collective_id=0, has_side_effects=True, vmem_limit_bytes=56 * 1024 * 1024
        ),
        name="grape",
    )(propagators[0, 0], target, weights)
    return summed[:, None, :]


def solution(mesh):
    placed = (P("ens", "tm", None, None), P("ens"), P())
    return jax.shard_map(
        shards, mesh=mesh, in_specs=placed, out_specs=P("ens", "tm", None), check_vma=False
    )
```

```python
import functools

import jax
import jax.numpy as jnp
from jax import lax
from jax.experimental import pallas as pl
from jax.experimental.pallas import tpu as pltpu
from jax.sharding import PartitionSpec as P

MESH = pl.DeviceIdType.MESH
R = 512
HALF = R // 2
PIECE = 128
SMALL = 64
SUB = 32
ROWS = 64
CHUNK = 16
COPIES = 160


def split(value):
    high = value.astype(jnp.bfloat16)
    low = (value - high.astype(jnp.float32)).astype(jnp.bfloat16)
    return high, low


def kernel(
    prop_ref, target_ref, weight_ref, out_ref,
    ends, target, mats, rows, strip, va, vb, mid, full, grad,
    long_in, short_in, bh, bl, send_sem, recv_sem, local_sem,
):
    slot = lax.axis_index("tm")
    z = lax.axis_index("ens")
    core = lax.rem(slot, 2)
    y = lax.rem(slot // 2, 4)
    x = slot // 8

    def at(x_, y_, core_):
        return ((x_ * 4 + y_) * 2 + core_, z)

    xp, xm, xo = lax.rem(x + 1, 4), lax.rem(x + 3, 4), lax.rem(x + 2, 4)
    yp, ym, yo = lax.rem(y + 1, 4), lax.rem(y + 3, 4), lax.rem(y + 2, 4)
    sibling = at(x, y, 1 - core)
    to_yp, to_ym = at(x, yp, core), at(x, ym, core)
    to_xp, to_xm = at(xp, y, core), at(xm, y, core)
    to_long = (slot, lax.rem(z + 1 + 6 * core, 8))
    to_short = (slot, lax.rem(z + 7 - 6 * core, 8))

    own_load = pltpu.make_async_copy(prop_ref, ends.at[core], local_sem.at[0])
    own_load.start()
    target_load = pltpu.make_async_copy(target_ref, target, local_sem.at[1])
    target_load.start()

    barrier = pltpu.get_barrier_semaphore()
    peers = (sibling, to_yp, to_ym, to_xp, to_xm, to_long, to_short)
    for peer in peers:
        pl.semaphore_signal(barrier, inc=1, device_id=peer, device_id_type=MESH)
    pl.semaphore_wait(barrier, len(peers))

    started = []

    def send(src, dst, device):
        n = len(started)
        copy = pltpu.make_async_remote_copy(
            src_ref=src, dst_ref=dst, send_sem=send_sem.at[n], recv_sem=recv_sem.at[n],
            device_id=device, device_id_type=MESH,
        )
        copy.start()
        started.append(copy)
        return copy

    def prepare(b):
        high, low = split(b[...])
        bh[...] = high
        bl[...] = low

    def product_rows(dst, a, start, count, nt=False):
        dims = (((1,), (1 if nt else 0,)), ((), ()))

        def dot(p, q):
            return lax.dot_general(p, q, dims, preferred_element_type=jnp.float32)

        block = pl.ds(start, count)
        high, low = split(a[block, :])
        dst[block, :] = dot(high, bh[...]) + (dot(high, bl[...]) + dot(low, bh[...]))

    def product(dst, a, b, nt=False):
        prepare(b)

        def one(i, _):
            product_rows(dst, a, pl.multiple_of(i * HALF, HALF), HALF, nt)
            return 0

        lax.fori_loop(0, 2, one, 0)

    swap = send(prop_ref, ends.at[core], sibling)
    own_load.wait()
    swap.wait_recv()
    mine = pl.multiple_of(core * HALF, HALF)
    other = pl.multiple_of((1 - core) * HALF, HALF)
    first, second = pl.ds(mine, PIECE), pl.ds(mine + PIECE, PIECE)
    prepare(ends.at[0])
    own = mats.at[y]
    product_rows(own, ends.at[1], mine, PIECE)
    up0 = send(own.at[first], own.at[first], to_yp)
    product_rows(own, ends.at[1], pl.multiple_of(mine + PIECE, PIECE), PIECE)
    down0 = send(own.at[second], own.at[second], to_ym)
    up1 = send(own.at[second], own.at[second], to_yp)
    down1 = send(own.at[first], own.at[first], to_ym)
    product_rows(own, ends.at[1], other, HALF)

    @pl.when(core == 1)
    def _():
        ends[0] = own[...]
        down = lax.broadcasted_iota(jnp.int32, (R, R), 0)
        across = lax.broadcasted_iota(jnp.int32, (R, R), 1)
        ends[1] = jnp.where(down == across, 1.0, 0.0).astype(jnp.float32)

    def pass_on(ref, block):
        return send(ref.at[block], ref.at[block], sibling)

    up0.wait_recv()
    up2 = send(mats.at[ym].at[first], mats.at[ym].at[first], to_yp)
    near = [pass_on(mats.at[ym], first)]
    down0.wait_recv()
    down2 = send(mats.at[yp].at[second], mats.at[yp].at[second], to_ym)
    near.append(pass_on(mats.at[yp], second))
    up1.wait_recv()
    near.append(pass_on(mats.at[ym], second))
    down1.wait_recv()
    near.append(pass_on(mats.at[yp], first))
    for copy in near:
        copy.wait_recv()
    late, odd = y // 2, lax.rem(y, 2)
    product(mats.at[4 + late], mats.at[2 * late + 1], mats.at[2 * late])

    @pl.when(odd == 0)
    def _():
        product(ends.at[2], mats.at[2 * late + 1], ends.at[1])

    @pl.when(odd == 1)
    def _():
        product(ends.at[2], ends.at[0], mats.at[2 * late])

    up2.wait_recv()
    far = [pass_on(mats.at[yo], first)]
    down2.wait_recv()
    far.append(pass_on(mats.at[yo], second))
    for copy in far:
        copy.wait_recv()

    subs = SMALL // SUB

    def pieces(half, number):
        start = half * HALF + number * SMALL
        return [pl.ds(pl.multiple_of(start + n * SUB, SUB), SUB) for n in range(subs)]

    a_here, b_here = pieces(odd, core), pieces(odd, 2 + core)
    a_there, b_there = pieces(1 - odd, core), pieces(1 - odd, 2 + core)
    begin = mats.at[3 + 2 * late]
    for n in range(subs):
        strip[n * SUB:(n + 1) * SUB, :] = begin[a_here[n], :]
        strip[SMALL + n * SUB:SMALL + (n + 1) * SUB, :] = begin[b_here[n], :]
    prepare(mats.at[2 - late])
    product_rows(strip, strip, 0, 2 * SMALL)
    prepare(mats.at[4 - 4 * late])
    product_rows(strip, strip, 0, 2 * SMALL)
    target_load.wait()

    @pl.when(x == 0)
    def _():
        prepare(target)
        product_rows(strip, strip, 0, 2 * SMALL, nt=True)

    strip_a = [strip.at[pl.ds(n * SUB, SUB)] for n in range(subs)]
    strip_b = [strip.at[pl.ds(SMALL + n * SUB, SUB)] for n in range(subs)]
    own_row = rows.at[x]
    xu_a, xd_b, xu_b, xd_a = [], [], [], []
    for n in range(subs):
        xu_a.append(send(strip_a[n], own_row.at[a_here[n]], to_xp))
        xd_b.append(send(strip_b[n], own_row.at[b_here[n]], to_xm))
    for n in range(subs):
        xu_b.append(send(strip_b[n], own_row.at[b_here[n]], to_xp))
        xd_a.append(send(strip_a[n], own_row.at[a_here[n]], to_xm))

    product(mats.at[5 - late], mats.at[3 - 2 * late], mats.at[2 - 2 * late])

    @pl.when(late == 0)
    def _():
        product(ends.at[3], mats.at[5], ends.at[2 - odd])

    @pl.when(late == 1)
    def _():
        product(ends.at[3], ends.at[2 * odd], mats.at[4])

    left = ends.at[(1 - late) * 2 * odd + late * 3]
    right = ends.at[(1 - late) * 3 + late * (2 - odd)]

    close_x, close_y, far_x, far_y = [], [], [], []
    onward, relays_u, relays_d = [], [], []

    def forward(copy, at_row, block, to_y, relay=None):
        copy.wait_recv()
        part = rows.at[at_row].at[block]
        relayed = None if relay is None else send(part, part, relay)
        return relayed, send(part, part, to_y), send(part, part, sibling)

    for n in range(subs):
        relayed, up, got = forward(xu_a[n], xm, a_here[n], to_yp, to_xp)
        relays_u.append(relayed)
        onward.append((up, xm, a_there[n]))
        close_x.append(got)
        relayed, up, got = forward(xd_b[n], xp, b_here[n], to_ym, to_xm)
        relays_d.append(relayed)
        onward.append((up, xp, b_there[n]))
        close_x.append(got)
    for n in range(subs):
        _, up, got = forward(xu_b[n], xm, b_here[n], to_ym)
        onward.append((up, xm, b_there[n]))
        close_x.append(got)
        _, up, got = forward(xd_a[n], xp, a_here[n], to_yp)
        onward.append((up, xp, a_there[n]))
        close_x.append(got)
    onward_far = []
    for n in range(subs):
        _, up, got = forward(relays_u[n], xo, a_here[n], to_yp)
        onward_far.append((up, a_there[n]))
        far_x.append(got)
        _, up, got = forward(relays_d[n], xo, b_here[n], to_ym)
        onward_far.append((up, b_there[n]))
        far_x.append(got)

    @pl.when(x == 0)
    def _():
        product(left, left, target, nt=True)

    def pass_some(some):
        for copy, at_row, block in some:
            copy.wait_recv()
            close_y.append(pass_on(rows.at[at_row], block))

    near_half = pl.multiple_of(odd * HALF, HALF)
    far_half = pl.multiple_of((1 - odd) * HALF, HALF)

    def add_half(dst, a, b, start, first):
        block = pl.ds(start, HALF)
        b_high, b_low = split(b[block, :])
        high, low = split(a[:, block])

        def dot(p, q):
            return jnp.dot(p, q, preferred_element_type=jnp.float32)

        value = dot(high, b_high) + (dot(high, b_low) + dot(low, b_high))
        dst[...] = value if first else dst[...] + value

    pass_some(onward[:2 * subs])
    for copy in close_x:
        copy.wait_recv()
    add_half(va, left, rows.at[xm], near_half, True)
    prepare(right)
    product_rows(vb, rows.at[xp], near_half, HALF)
    pass_some(onward[2 * subs:])
    for copy in close_y:
        copy.wait_recv()
    add_half(va, left, rows.at[xm], far_half, False)
    product_rows(vb, rows.at[xp], far_half, HALF)
    for copy, block in onward_far:
        copy.wait_recv()
        far_y.append(pass_on(rows.at[xo], block))
    for copy in far_x:
        copy.wait_recv()
    prepare(vb)
    product_rows(mid, rows.at[xo], near_half, HALF)
    add_half(full, va, mid, near_half, True)
    for copy in far_y:
        copy.wait_recv()
    product_rows(mid, rows.at[xo], far_half, HALF)
    add_half(full, va, mid, far_half, False)
    scale = 0.5 * weight_ref[0]
    turned = full[...]
    grad[...] = scale * (turned - turned.T)

    chunks = ROWS // CHUNK

    def own_rows(owner, q):
        return pl.ds(pl.multiple_of(owner * ROWS + q * CHUNK, CHUNK), CHUNK)

    def owner_long(step):
        return lax.rem(z + (4 - step) + core * 2 * (4 + step), 8)

    def owner_short(step):
        return lax.rem(z + 5 + step + core * 2 * (3 - step), 8)

    def hop(copies, step, q, owner, landed, device):
        spot = pl.ds(q * CHUNK, CHUNK)
        block = own_rows(owner(step), q)
        if step == 0:
            src = grad.at[block]
        else:
            copies[(step - 1) * chunks + q].wait_recv()
            src = landed.at[step - 1].at[spot]
            src[...] += grad[block, :]
        copies.append(send(src, landed.at[step].at[spot], device))

    long_copies, short_copies = [], []
    for step in range(4):
        for q in range(chunks):
            hop(long_copies, step, q, owner_long, long_in, to_long)
        if step < 3:
            for q in range(chunks):
                hop(short_copies, step, q, owner_short, short_in, to_short)
    for q in range(chunks):
        spot = pl.ds(q * CHUNK, CHUNK)
        short_copies[2 * chunks + q].wait_recv()
        long_copies[3 * chunks + q].wait_recv()
        out_ref[spot, :] = (
            grad[own_rows(z, q), :] + long_in[3, spot, :] + short_in[2, spot, :]
        )
    for copy in started:
        copy.wait_send()
    assert len(started) <= COPIES


def shards(propagators, weights, target):
    full = pltpu.VMEM((R, R), jnp.float32)
    summed = pl.pallas_call(
        kernel,
        out_shape=jax.ShapeDtypeStruct((ROWS, R), jnp.float32),
        in_specs=[
            pl.BlockSpec(memory_space=pl.ANY),
            pl.BlockSpec(memory_space=pl.ANY),
            pl.BlockSpec(memory_space=pltpu.SMEM),
        ],
        out_specs=pl.BlockSpec(memory_space=pltpu.VMEM),
        scratch_shapes=[
            pltpu.VMEM((4, R, R), jnp.float32),
            full,
            pltpu.VMEM((6, R, R), jnp.float32),
            pltpu.VMEM((4, R, R), jnp.float32),
            pltpu.VMEM((2 * SMALL, R), jnp.float32),
            full, full, full, full, full,
            pltpu.VMEM((4, ROWS, R), jnp.float32),
            pltpu.VMEM((3, ROWS, R), jnp.float32),
            pltpu.VMEM((R, R), jnp.bfloat16),
            pltpu.VMEM((R, R), jnp.bfloat16),
            pltpu.SemaphoreType.DMA((COPIES,)),
            pltpu.SemaphoreType.DMA((COPIES,)),
            pltpu.SemaphoreType.DMA((2,)),
        ],
        compiler_params=pltpu.CompilerParams(
            collective_id=0, has_side_effects=True, vmem_limit_bytes=53 * 1024 * 1024
        ),
        name="grape",
    )(propagators[0, 0], target, weights)
    return summed[:, None, :]


def solution(mesh):
    placed = (P("ens", "tm", None, None), P("ens"), P())
    return jax.shard_map(
        shards, mesh=mesh, in_specs=placed, out_specs=P("ens", "tm", None), check_vma=False
    )
```

```python
import functools

import jax
import jax.numpy as jnp
from jax import lax
from jax.experimental import pallas as pl
from jax.experimental.pallas import tpu as pltpu
from jax.sharding import PartitionSpec as P

MESH = pl.DeviceIdType.MESH
R = 512
HALF = R // 2
PIECE = 128
SMALL = 64
SUB = 32
ROWS = 64
CHUNK = 8
COPIES = 160


def split(value):
    high = value.astype(jnp.bfloat16)
    low = (value - high.astype(jnp.float32)).astype(jnp.bfloat16)
    return high, low


def kernel(
    prop_ref, target_ref, weight_ref, out_ref,
    ends, target, mats, rows, strip, va, vb, mid, full, grad,
    long_in, short_in, bh, bl, send_sem, recv_sem, local_sem,
):
    slot = lax.axis_index("tm")
    z = lax.axis_index("ens")
    core = lax.rem(slot, 2)
    y = lax.rem(slot // 2, 4)
    x = slot // 8

    def at(x_, y_, core_):
        return ((x_ * 4 + y_) * 2 + core_, z)

    xp, xm, xo = lax.rem(x + 1, 4), lax.rem(x + 3, 4), lax.rem(x + 2, 4)
    yp, ym, yo = lax.rem(y + 1, 4), lax.rem(y + 3, 4), lax.rem(y + 2, 4)
    sibling = at(x, y, 1 - core)
    to_yp, to_ym = at(x, yp, core), at(x, ym, core)
    to_xp, to_xm = at(xp, y, core), at(xm, y, core)
    to_long = (slot, lax.rem(z + 1 + 6 * core, 8))
    to_short = (slot, lax.rem(z + 7 - 6 * core, 8))

    own_load = pltpu.make_async_copy(prop_ref, ends.at[core], local_sem.at[0])
    own_load.start()
    target_load = pltpu.make_async_copy(target_ref, target, local_sem.at[1])
    target_load.start()

    barrier = pltpu.get_barrier_semaphore()
    peers = (sibling, to_yp, to_ym, to_xp, to_xm, to_long, to_short)
    for peer in peers:
        pl.semaphore_signal(barrier, inc=1, device_id=peer, device_id_type=MESH)
    pl.semaphore_wait(barrier, len(peers))

    started = []

    def send(src, dst, device):
        n = len(started)
        copy = pltpu.make_async_remote_copy(
            src_ref=src, dst_ref=dst, send_sem=send_sem.at[n], recv_sem=recv_sem.at[n],
            device_id=device, device_id_type=MESH,
        )
        copy.start()
        started.append(copy)
        return copy

    def prepare(b, spot=0):
        high, low = split(b[...])
        bh[spot] = high
        bl[spot] = low

    def product_rows(dst, a, start, count, nt=False, spot=0):
        dims = (((1,), (1 if nt else 0,)), ((), ()))

        def dot(p, q):
            return lax.dot_general(p, q, dims, preferred_element_type=jnp.float32)

        block = pl.ds(start, count)
        high, low = split(a[block, :])
        dst[block, :] = dot(high, bh[spot]) + (dot(high, bl[spot]) + dot(low, bh[spot]))

    def product(dst, a, b, nt=False):
        prepare(b)

        def one(i, _):
            product_rows(dst, a, pl.multiple_of(i * HALF, HALF), HALF, nt)
            return 0

        lax.fori_loop(0, 2, one, 0)

    swap = send(prop_ref, ends.at[core], sibling)
    own_load.wait()
    swap.wait_recv()
    mine = pl.multiple_of(core * HALF, HALF)
    other = pl.multiple_of((1 - core) * HALF, HALF)
    first, second = pl.ds(mine, PIECE), pl.ds(mine + PIECE, PIECE)
    prepare(ends.at[0])
    own = mats.at[y]
    product_rows(own, ends.at[1], mine, PIECE)
    up0 = send(own.at[first], own.at[first], to_yp)
    product_rows(own, ends.at[1], pl.multiple_of(mine + PIECE, PIECE), PIECE)
    down0 = send(own.at[second], own.at[second], to_ym)
    up1 = send(own.at[second], own.at[second], to_yp)
    down1 = send(own.at[first], own.at[first], to_ym)
    product_rows(own, ends.at[1], other, HALF)

    @pl.when(core == 1)
    def _():
        ends[0] = own[...]
        down = lax.broadcasted_iota(jnp.int32, (R, R), 0)
        across = lax.broadcasted_iota(jnp.int32, (R, R), 1)
        ends[1] = jnp.where(down == across, 1.0, 0.0).astype(jnp.float32)

    def pass_on(ref, block):
        return send(ref.at[block], ref.at[block], sibling)

    up0.wait_recv()
    up2 = send(mats.at[ym].at[first], mats.at[ym].at[first], to_yp)
    near = [pass_on(mats.at[ym], first)]
    down0.wait_recv()
    down2 = send(mats.at[yp].at[second], mats.at[yp].at[second], to_ym)
    near.append(pass_on(mats.at[yp], second))
    up1.wait_recv()
    near.append(pass_on(mats.at[ym], second))
    down1.wait_recv()
    near.append(pass_on(mats.at[yp], first))
    for copy in near:
        copy.wait_recv()
    late, odd = y // 2, lax.rem(y, 2)
    product(mats.at[4 + late], mats.at[2 * late + 1], mats.at[2 * late])

    @pl.when(odd == 0)
    def _():
        product(ends.at[2], mats.at[2 * late + 1], ends.at[1])

    @pl.when(odd == 1)
    def _():
        product(ends.at[2], ends.at[0], mats.at[2 * late])

    subs = SMALL // SUB

    def pieces(half, number):
        start = half * HALF + number * SMALL
        return [pl.ds(pl.multiple_of(start + n * SUB, SUB), SUB) for n in range(subs)]

    a_here, b_here = pieces(odd, core), pieces(odd, 2 + core)
    a_there, b_there = pieces(1 - odd, core), pieces(1 - odd, 2 + core)
    begin = mats.at[3 + 2 * late]
    third = y == 2

    def gather_strip():
        for n in range(subs):
            strip[n * SUB:(n + 1) * SUB, :] = begin[a_here[n], :]
            strip[SMALL + n * SUB:SMALL + (n + 1) * SUB, :] = begin[b_here[n], :]

    prepare(mats.at[(1 - late) * 4 + late * (1 - odd)], 1)
    target_load.wait()
    prepare(target, 2)

    @pl.when(third)
    def _():
        gather_strip()
        product_rows(strip, strip, 0, 2 * SMALL, spot=1)

    up2.wait_recv()
    far = [pass_on(mats.at[yo], first)]
    down2.wait_recv()
    far.append(pass_on(mats.at[yo], second))
    for copy in far:
        copy.wait_recv()

    @pl.when(third)
    def _():
        prepare(mats.at[0])
        product_rows(strip, strip, 0, 2 * SMALL)

    @pl.when(jnp.logical_not(third))
    def _():
        prepare(mats.at[2 - late])
        gather_strip()
        product_rows(strip, strip, 0, 2 * SMALL)
        product_rows(strip, strip, 0, 2 * SMALL, spot=1)

    @pl.when(x == 0)
    def _():
        product_rows(strip, strip, 0, 2 * SMALL, nt=True, spot=2)

    strip_a = [strip.at[pl.ds(n * SUB, SUB)] for n in range(subs)]
    strip_b = [strip.at[pl.ds(SMALL + n * SUB, SUB)] for n in range(subs)]
    own_row = rows.at[x]
    xu_a, xd_b, xu_b, xd_a = [], [], [], []
    for n in range(subs):
        xu_a.append(send(strip_a[n], own_row.at[a_here[n]], to_xp))
        xd_b.append(send(strip_b[n], own_row.at[b_here[n]], to_xm))
    for n in range(subs):
        xu_b.append(send(strip_b[n], own_row.at[b_here[n]], to_xp))
        xd_a.append(send(strip_a[n], own_row.at[a_here[n]], to_xm))

    product(mats.at[5 - late], mats.at[3 - 2 * late], mats.at[2 - 2 * late])

    @pl.when(late == 0)
    def _():
        product(ends.at[3], mats.at[5], ends.at[2 - odd])

    @pl.when(late == 1)
    def _():
        product(ends.at[3], ends.at[2 * odd], mats.at[4])

    left = ends.at[(1 - late) * 2 * odd + late * 3]
    right = ends.at[(1 - late) * 3 + late * (2 - odd)]

    close_x, close_y, far_x, far_y = [], [], [], []
    onward, relays_u, relays_d = [], [], []

    def forward(copy, at_row, block, to_y, relay=None):
        copy.wait_recv()
        part = rows.at[at_row].at[block]
        relayed = None if relay is None else send(part, part, relay)
        return relayed, send(part, part, to_y), send(part, part, sibling)

    for n in range(subs):
        relayed, up, got = forward(xu_a[n], xm, a_here[n], to_yp, to_xp)
        relays_u.append(relayed)
        onward.append((up, xm, a_there[n]))
        close_x.append(got)
        relayed, up, got = forward(xd_b[n], xp, b_here[n], to_ym, to_xm)
        relays_d.append(relayed)
        onward.append((up, xp, b_there[n]))
        close_x.append(got)
    for n in range(subs):
        _, up, got = forward(xu_b[n], xm, b_here[n], to_ym)
        onward.append((up, xm, b_there[n]))
        close_x.append(got)
        _, up, got = forward(xd_a[n], xp, a_here[n], to_yp)
        onward.append((up, xp, a_there[n]))
        close_x.append(got)
    onward_far = []
    for n in range(subs):
        _, up, got = forward(relays_u[n], xo, a_here[n], to_yp)
        onward_far.append((up, a_there[n]))
        far_x.append(got)
        _, up, got = forward(relays_d[n], xo, b_here[n], to_ym)
        onward_far.append((up, b_there[n]))
        far_x.append(got)

    @pl.when(x == 0)
    def _():
        product(left, left, target, nt=True)

    def pass_some(some):
        for copy, at_row, block in some:
            copy.wait_recv()
            close_y.append(pass_on(rows.at[at_row], block))

    near_half = pl.multiple_of(odd * HALF, HALF)
    far_half = pl.multiple_of((1 - odd) * HALF, HALF)

    def add_half(dst, a, b, start, first):
        block = pl.ds(start, HALF)
        b_high, b_low = split(b[block, :])
        high, low = split(a[:, block])

        def dot(p, q):
            return jnp.dot(p, q, preferred_element_type=jnp.float32)

        value = dot(high, b_high) + (dot(high, b_low) + dot(low, b_high))
        dst[...] = value if first else dst[...] + value

    pass_some(onward[:2 * subs])
    for copy in close_x:
        copy.wait_recv()
    add_half(va, left, rows.at[xm], near_half, True)
    prepare(right)
    product_rows(vb, rows.at[xp], near_half, HALF)
    pass_some(onward[2 * subs:])
    for copy in close_y:
        copy.wait_recv()
    add_half(va, left, rows.at[xm], far_half, False)
    product_rows(vb, rows.at[xp], far_half, HALF)
    for copy, block in onward_far:
        copy.wait_recv()
        far_y.append(pass_on(rows.at[xo], block))
    for copy in far_x:
        copy.wait_recv()
    prepare(vb)
    product_rows(mid, rows.at[xo], near_half, HALF)
    add_half(full, va, mid, near_half, True)
    for copy in far_y:
        copy.wait_recv()
    product_rows(mid, rows.at[xo], far_half, HALF)
    add_half(full, va, mid, far_half, False)
    scale = 0.5 * weight_ref[0]
    turned = full[...]
    grad[...] = scale * (turned - turned.T)

    chunks = ROWS // CHUNK

    def own_rows(owner, q):
        return pl.ds(pl.multiple_of(owner * ROWS + q * CHUNK, CHUNK), CHUNK)

    def owner_long(step):
        return lax.rem(z + (4 - step) + core * 2 * (4 + step), 8)

    def owner_short(step):
        return lax.rem(z + 5 + step + core * 2 * (3 - step), 8)

    def hop(copies, step, q, owner, landed, device):
        spot = pl.ds(q * CHUNK, CHUNK)
        block = own_rows(owner(step), q)
        if step == 0:
            src = grad.at[block]
        else:
            copies[(step - 1) * chunks + q].wait_recv()
            src = landed.at[step - 1].at[spot]
            src[...] += grad[block, :]
        copies.append(send(src, landed.at[step].at[spot], device))

    long_copies, short_copies = [], []
    for step in range(4):
        for q in range(chunks):
            hop(long_copies, step, q, owner_long, long_in, to_long)
        if step < 3:
            for q in range(chunks):
                hop(short_copies, step, q, owner_short, short_in, to_short)
    for q in range(chunks):
        spot = pl.ds(q * CHUNK, CHUNK)
        short_copies[2 * chunks + q].wait_recv()
        long_copies[3 * chunks + q].wait_recv()
        out_ref[spot, :] = (
            grad[own_rows(z, q), :] + long_in[3, spot, :] + short_in[2, spot, :]
        )
    for copy in started:
        copy.wait_send()
    assert len(started) <= COPIES


def shards(propagators, weights, target):
    full = pltpu.VMEM((R, R), jnp.float32)
    summed = pl.pallas_call(
        kernel,
        out_shape=jax.ShapeDtypeStruct((ROWS, R), jnp.float32),
        in_specs=[
            pl.BlockSpec(memory_space=pl.ANY),
            pl.BlockSpec(memory_space=pl.ANY),
            pl.BlockSpec(memory_space=pltpu.SMEM),
        ],
        out_specs=pl.BlockSpec(memory_space=pltpu.VMEM),
        scratch_shapes=[
            pltpu.VMEM((4, R, R), jnp.float32),
            full,
            pltpu.VMEM((6, R, R), jnp.float32),
            pltpu.VMEM((4, R, R), jnp.float32),
            pltpu.VMEM((2 * SMALL, R), jnp.float32),
            full, full, full, full, full,
            pltpu.VMEM((4, ROWS, R), jnp.float32),
            pltpu.VMEM((3, ROWS, R), jnp.float32),
            pltpu.VMEM((3, R, R), jnp.bfloat16),
            pltpu.VMEM((3, R, R), jnp.bfloat16),
            pltpu.SemaphoreType.DMA((COPIES,)),
            pltpu.SemaphoreType.DMA((COPIES,)),
            pltpu.SemaphoreType.DMA((2,)),
        ],
        compiler_params=pltpu.CompilerParams(
            collective_id=0, has_side_effects=True, vmem_limit_bytes=53 * 1024 * 1024
        ),
        name="grape",
    )(propagators[0, 0], target, weights)
    return summed[:, None, :]


def solution(mesh):
    placed = (P("ens", "tm", None, None), P("ens"), P())
    return jax.shard_map(
        shards, mesh=mesh, in_specs=placed, out_specs=P("ens", "tm", None), check_vma=False
    )
```

```python
import functools

import jax
import jax.numpy as jnp
from jax import lax
from jax.experimental import pallas as pl
from jax.experimental.pallas import tpu as pltpu
from jax.sharding import PartitionSpec as P

MESH = pl.DeviceIdType.MESH
R = 512
HALF = R // 2
PIECE = 128
SMALL = 64
SUB = 32
ROWS = 64
CHUNK = 8
COPIES = 160


def split(value):
    high = value.astype(jnp.bfloat16)
    low = (value - high.astype(jnp.float32)).astype(jnp.bfloat16)
    return high, low


def kernel(
    prop_ref, target_ref, weight_ref, out_ref,
    ends, target, mats, rows, strip, va, vb, mid, full, grad,
    long_in, short_in, bh, bl, send_sem, recv_sem, local_sem,
):
    slot = lax.axis_index("tm")
    z = lax.axis_index("ens")
    core = lax.rem(slot, 2)
    y = lax.rem(slot // 2, 4)
    x = slot // 8

    def at(x_, y_, core_):
        return ((x_ * 4 + y_) * 2 + core_, z)

    xp, xm, xo = lax.rem(x + 1, 4), lax.rem(x + 3, 4), lax.rem(x + 2, 4)
    yp, ym, yo = lax.rem(y + 1, 4), lax.rem(y + 3, 4), lax.rem(y + 2, 4)
    sibling = at(x, y, 1 - core)
    to_yp, to_ym = at(x, yp, core), at(x, ym, core)
    to_xp, to_xm = at(xp, y, core), at(xm, y, core)
    to_long = (slot, lax.rem(z + 1 + 6 * core, 8))
    to_short = (slot, lax.rem(z + 7 - 6 * core, 8))

    own_load = pltpu.make_async_copy(prop_ref, ends.at[core], local_sem.at[0])
    own_load.start()
    target_load = pltpu.make_async_copy(target_ref, target, local_sem.at[1])

    barrier = pltpu.get_barrier_semaphore()
    peers = (sibling, to_yp, to_ym, to_xp, to_xm, to_long, to_short)
    for peer in peers:
        pl.semaphore_signal(barrier, inc=1, device_id=peer, device_id_type=MESH)
    pl.semaphore_wait(barrier, len(peers))

    started = []

    def send(src, dst, device):
        n = len(started)
        copy = pltpu.make_async_remote_copy(
            src_ref=src, dst_ref=dst, send_sem=send_sem.at[n], recv_sem=recv_sem.at[n],
            device_id=device, device_id_type=MESH,
        )
        copy.start()
        started.append(copy)
        return copy

    def prepare(b, spot=0):
        high, low = split(b[...])
        bh[spot] = high
        bl[spot] = low

    def product_rows(dst, a, start, count, nt=False, spot=0):
        dims = (((1,), (1 if nt else 0,)), ((), ()))

        def dot(p, q):
            return lax.dot_general(p, q, dims, preferred_element_type=jnp.float32)

        block = pl.ds(start, count)
        high, low = split(a[block, :])
        dst[block, :] = dot(high, bh[spot]) + (dot(high, bl[spot]) + dot(low, bh[spot]))

    def product(dst, a, b, nt=False):
        prepare(b)

        def one(i, _):
            product_rows(dst, a, pl.multiple_of(i * HALF, HALF), HALF, nt)
            return 0

        lax.fori_loop(0, 2, one, 0)

    swap = send(prop_ref, ends.at[core], sibling)
    own_load.wait()
    swap.wait_recv()
    target_load.start()
    mine = pl.multiple_of(core * HALF, HALF)
    other = pl.multiple_of((1 - core) * HALF, HALF)
    first, second = pl.ds(mine, PIECE), pl.ds(mine + PIECE, PIECE)
    prepare(ends.at[0])
    own = mats.at[y]
    product_rows(own, ends.at[1], mine, PIECE)
    up0 = send(own.at[first], own.at[first], to_yp)
    product_rows(own, ends.at[1], pl.multiple_of(mine + PIECE, PIECE), PIECE)
    down0 = send(own.at[second], own.at[second], to_ym)
    up1 = send(own.at[second], own.at[second], to_yp)
    down1 = send(own.at[first], own.at[first], to_ym)
    product_rows(own, ends.at[1], other, HALF)

    @pl.when(core == 1)
    def _():
        ends[0] = own[...]
        down = lax.broadcasted_iota(jnp.int32, (R, R), 0)
        across = lax.broadcasted_iota(jnp.int32, (R, R), 1)
        ends[1] = jnp.where(down == across, 1.0, 0.0).astype(jnp.float32)

    def pass_on(ref, block):
        return send(ref.at[block], ref.at[block], sibling)

    up0.wait_recv()
    up2 = send(mats.at[ym].at[first], mats.at[ym].at[first], to_yp)
    near = [pass_on(mats.at[ym], first)]
    down0.wait_recv()
    down2 = send(mats.at[yp].at[second], mats.at[yp].at[second], to_ym)
    near.append(pass_on(mats.at[yp], second))
    up1.wait_recv()
    near.append(pass_on(mats.at[ym], second))
    down1.wait_recv()
    near.append(pass_on(mats.at[yp], first))
    for copy in near:
        copy.wait_recv()
    late, odd = y // 2, lax.rem(y, 2)
    product(mats.at[4 + late], mats.at[2 * late + 1], mats.at[2 * late])

    @pl.when(odd == 0)
    def _():
        product(ends.at[2], mats.at[2 * late + 1], ends.at[1])

    @pl.when(odd == 1)
    def _():
        product(ends.at[2], ends.at[0], mats.at[2 * late])

    subs = SMALL // SUB

    def pieces(half, number):
        start = half * HALF + number * SMALL
        return [pl.ds(pl.multiple_of(start + n * SUB, SUB), SUB) for n in range(subs)]

    a_here, b_here = pieces(odd, core), pieces(odd, 2 + core)
    a_there, b_there = pieces(1 - odd, core), pieces(1 - odd, 2 + core)
    begin = mats.at[3 + 2 * late]
    third = y == 2

    def gather_strip():
        for n in range(subs):
            strip[n * SUB:(n + 1) * SUB, :] = begin[a_here[n], :]
            strip[SMALL + n * SUB:SMALL + (n + 1) * SUB, :] = begin[b_here[n], :]

    prepare(mats.at[(1 - late) * 4 + late * (1 - odd)], 1)
    target_load.wait()
    prepare(target, 2)

    @pl.when(third)
    def _():
        gather_strip()
        product_rows(strip, strip, 0, 2 * SMALL, spot=1)

    up2.wait_recv()
    far = [pass_on(mats.at[yo], first)]
    down2.wait_recv()
    far.append(pass_on(mats.at[yo], second))
    for copy in far:
        copy.wait_recv()

    @pl.when(third)
    def _():
        prepare(mats.at[0])
        product_rows(strip, strip, 0, 2 * SMALL)

    @pl.when(jnp.logical_not(third))
    def _():
        prepare(mats.at[2 - late])
        gather_strip()
        product_rows(strip, strip, 0, 2 * SMALL)
        product_rows(strip, strip, 0, 2 * SMALL, spot=1)

    @pl.when(x == 0)
    def _():
        product_rows(strip, strip, 0, 2 * SMALL, nt=True, spot=2)

    strip_a = [strip.at[pl.ds(n * SUB, SUB)] for n in range(subs)]
    strip_b = [strip.at[pl.ds(SMALL + n * SUB, SUB)] for n in range(subs)]
    own_row = rows.at[x]
    xu_a, xd_b, xu_b, xd_a = [], [], [], []
    for n in range(subs):
        xu_a.append(send(strip_a[n], own_row.at[a_here[n]], to_xp))
        xd_b.append(send(strip_b[n], own_row.at[b_here[n]], to_xm))
    for n in range(subs):
        xu_b.append(send(strip_b[n], own_row.at[b_here[n]], to_xp))
        xd_a.append(send(strip_a[n], own_row.at[a_here[n]], to_xm))

    product(mats.at[5 - late], mats.at[3 - 2 * late], mats.at[2 - 2 * late])

    @pl.when(late == 0)
    def _():
        product(ends.at[3], mats.at[5], ends.at[2 - odd])

    @pl.when(late == 1)
    def _():
        product(ends.at[3], ends.at[2 * odd], mats.at[4])

    left = ends.at[(1 - late) * 2 * odd + late * 3]
    right = ends.at[(1 - late) * 3 + late * (2 - odd)]

    close_x, close_y, far_x, far_y = [], [], [], []
    onward, relays_u, relays_d = [], [], []

    def forward(copy, at_row, block, to_y, relay=None):
        copy.wait_recv()
        part = rows.at[at_row].at[block]
        relayed = None if relay is None else send(part, part, relay)
        return relayed, send(part, part, to_y), send(part, part, sibling)

    for n in range(subs):
        relayed, up, got = forward(xu_a[n], xm, a_here[n], to_yp, to_xp)
        relays_u.append(relayed)
        onward.append((up, xm, a_there[n]))
        close_x.append(got)
        relayed, up, got = forward(xd_b[n], xp, b_here[n], to_ym, to_xm)
        relays_d.append(relayed)
        onward.append((up, xp, b_there[n]))
        close_x.append(got)
    for n in range(subs):
        _, up, got = forward(xu_b[n], xm, b_here[n], to_ym)
        onward.append((up, xm, b_there[n]))
        close_x.append(got)
        _, up, got = forward(xd_a[n], xp, a_here[n], to_yp)
        onward.append((up, xp, a_there[n]))
        close_x.append(got)
    onward_far = []
    for n in range(subs):
        _, up, got = forward(relays_u[n], xo, a_here[n], to_yp)
        onward_far.append((up, a_there[n]))
        far_x.append(got)
        _, up, got = forward(relays_d[n], xo, b_here[n], to_ym)
        onward_far.append((up, b_there[n]))
        far_x.append(got)

    @pl.when(x == 0)
    def _():
        product(left, left, target, nt=True)

    def pass_some(some):
        for copy, at_row, block in some:
            copy.wait_recv()
            close_y.append(pass_on(rows.at[at_row], block))

    near_half = pl.multiple_of(odd * HALF, HALF)
    far_half = pl.multiple_of((1 - odd) * HALF, HALF)

    def add_half(dst, a, b, start, first):
        block = pl.ds(start, HALF)
        b_high, b_low = split(b[block, :])
        high, low = split(a[:, block])

        def dot(p, q):
            return jnp.dot(p, q, preferred_element_type=jnp.float32)

        value = dot(high, b_high) + (dot(high, b_low) + dot(low, b_high))
        dst[...] = value if first else dst[...] + value

    pass_some(onward[:2 * subs])
    for copy in close_x:
        copy.wait_recv()
    add_half(va, left, rows.at[xm], near_half, True)
    prepare(right)
    product_rows(vb, rows.at[xp], near_half, HALF)
    pass_some(onward[2 * subs:])
    for copy in close_y:
        copy.wait_recv()
    add_half(va, left, rows.at[xm], far_half, False)
    product_rows(vb, rows.at[xp], far_half, HALF)
    for copy, block in onward_far:
        copy.wait_recv()
        far_y.append(pass_on(rows.at[xo], block))
    for copy in far_x:
        copy.wait_recv()
    prepare(vb)
    product_rows(mid, rows.at[xo], near_half, HALF)
    add_half(full, va, mid, near_half, True)
    for copy in far_y:
        copy.wait_recv()
    product_rows(mid, rows.at[xo], far_half, HALF)
    add_half(full, va, mid, far_half, False)
    scale = 0.5 * weight_ref[0]
    turned = full[...]
    grad[...] = scale * (turned - turned.T)

    chunks = ROWS // CHUNK

    def own_rows(owner, q):
        return pl.ds(pl.multiple_of(owner * ROWS + q * CHUNK, CHUNK), CHUNK)

    def owner_long(step):
        return lax.rem(z + (4 - step) + core * 2 * (4 + step), 8)

    def owner_short(step):
        return lax.rem(z + 5 + step + core * 2 * (3 - step), 8)

    def hop(copies, step, q, owner, landed, device):
        spot = pl.ds(q * CHUNK, CHUNK)
        block = own_rows(owner(step), q)
        if step == 0:
            src = grad.at[block]
        else:
            copies[(step - 1) * chunks + q].wait_recv()
            src = landed.at[step - 1].at[spot]
            src[...] += grad[block, :]
        copies.append(send(src, landed.at[step].at[spot], device))

    long_copies, short_copies = [], []
    for step in range(4):
        for q in range(chunks):
            hop(long_copies, step, q, owner_long, long_in, to_long)
        if step < 3:
            for q in range(chunks):
                hop(short_copies, step, q, owner_short, short_in, to_short)
    for q in range(chunks):
        spot = pl.ds(q * CHUNK, CHUNK)
        short_copies[2 * chunks + q].wait_recv()
        long_copies[3 * chunks + q].wait_recv()
        out_ref[spot, :] = (
            grad[own_rows(z, q), :] + long_in[3, spot, :] + short_in[2, spot, :]
        )
    for copy in started:
        copy.wait_send()
    assert len(started) <= COPIES


def shards(propagators, weights, target):
    full = pltpu.VMEM((R, R), jnp.float32)
    summed = pl.pallas_call(
        kernel,
        out_shape=jax.ShapeDtypeStruct((ROWS, R), jnp.float32),
        in_specs=[
            pl.BlockSpec(memory_space=pl.ANY),
            pl.BlockSpec(memory_space=pl.ANY),
            pl.BlockSpec(memory_space=pltpu.SMEM),
        ],
        out_specs=pl.BlockSpec(memory_space=pltpu.VMEM),
        scratch_shapes=[
            pltpu.VMEM((4, R, R), jnp.float32),
            full,
            pltpu.VMEM((6, R, R), jnp.float32),
            pltpu.VMEM((4, R, R), jnp.float32),
            pltpu.VMEM((2 * SMALL, R), jnp.float32),
            full, full, full, full, full,
            pltpu.VMEM((4, ROWS, R), jnp.float32),
            pltpu.VMEM((3, ROWS, R), jnp.float32),
            pltpu.VMEM((3, R, R), jnp.bfloat16),
            pltpu.VMEM((3, R, R), jnp.bfloat16),
            pltpu.SemaphoreType.DMA((COPIES,)),
            pltpu.SemaphoreType.DMA((COPIES,)),
            pltpu.SemaphoreType.DMA((2,)),
        ],
        compiler_params=pltpu.CompilerParams(
            collective_id=0, has_side_effects=True, vmem_limit_bytes=53 * 1024 * 1024
        ),
        name="grape",
    )(propagators[0, 0], target, weights)
    return summed[:, None, :]


def solution(mesh):
    placed = (P("ens", "tm", None, None), P("ens"), P())
    return jax.shard_map(
        shards, mesh=mesh, in_specs=placed, out_specs=P("ens", "tm", None), check_vma=False
    )
```
